32 devices in a mesh: slab: 8 (over z, core), cross: 4 (over y, x).
Axes of the slice: x: 2, y: 2, z: 4, core: 2. Of those that a mesh axis runs over, the one named last changes fastest.
Arguments:
- forcing: float32 [2, 32, 256, 512], P(None, 'slab', 'cross'), may hold values from -6 to 6
- viscosity: float32 [32, 256, 512], P('slab', 'cross'), may hold values from 0.1 to 10
- owner_slot: int32 [512], replicated, may hold values from 0 to 511, each once
Outputs:
- velocity: float32 [2, 32, 256, 512], P(None, 'slab', 'cross')
- pressure: float32 [32, 512], P('slab', 'cross')
The draws below stay inside these ranges and needn't reach their ends.
All inputs are finite; a program needn't handle non-finite values.
Results may differ from the reference program's by a relative error of at most 0.00013.
Values sent between devices are 32-bit elements; how exact they have to be, the bound alone decides.
A program may use at most 64 MiB of HBM per device.

```python
import math
import jax
import jax.numpy as jnp

NZ = 512
OUTER = 2
DEGREE = 3
NX = 32
NY = 256


def draw_forcing(key, part):
    first = jax.random.fold_in(key, 0)
    ramp = 1.0 + 2.0 * jnp.arange(NX, dtype=jnp.float32) / max(NX - 1, 1)
    base = jnp.clip(jax.random.normal(first, (2, NX, NY, NZ), jnp.float32), -2.0, 2.0)
    return base * ramp[None, :, None, None]


def block_scale(key, extent, cuts, low, largest):
    level, own = 1.0, jax.random.fold_in(key, 6)
    for position, parts in cuts:
        heights = jnp.exp(jax.random.uniform(jax.random.fold_in(own, position), (parts,), jnp.float32, low / len(cuts), largest / len(cuts)))
        level = level * jnp.repeat(heights, extent[position] // parts).reshape([-1 if axis == position else 1 for axis in range(len(extent))])
    return level


def setup_inputs(seed: int = 0) -> dict:
    keys = jax.random.split(jax.random.key(seed), 4)
    return {
        "forcing": draw_forcing(jax.random.fold_in(keys[3], 71), 0),
        "viscosity": jnp.clip(jnp.exp(math.log(10.0) - 4.6051702 * jax.random.uniform(keys[1], (NX, NY, NZ), jnp.float32) ** block_scale(keys[1], (NX, NY, NZ), ((0, 8), (1, 4)), -0.2, 0.2)), 0.1, 10.0),
        "owner_slot": jax.random.permutation(keys[2], NZ).astype(jnp.int32),
    }


cheb_theta = 1.025
cheb_delta = 0.975


def face_parts(viscosity):
    rim = jnp.pad(viscosity, 1)
    centre = rim[1:-1, 1:-1, 1:-1]
    neighbours = [rim[2:, 1:-1, 1:-1], rim[:-2, 1:-1, 1:-1], rim[1:-1, 2:, 1:-1], rim[1:-1, :-2, 1:-1], rim[1:-1, 1:-1, 2:], rim[1:-1, 1:-1, :-2]]
    faces = [0.5 * (centre + nb) for nb in neighbours]
    diag = faces[0] + faces[1] + faces[2] + faces[3] + faces[4] + faces[5]
    return faces, diag


def apply_op(field, faces):
    padded = jnp.pad(field, ((0, 0), (1, 1), (1, 1), (1, 1)))
    neighbours = [padded[:, 2:, 1:-1, 1:-1], padded[:, :-2, 1:-1, 1:-1], padded[:, 1:-1, 2:, 1:-1], padded[:, 1:-1, :-2, 1:-1], padded[:, 1:-1, 1:-1, 2:], padded[:, 1:-1, 1:-1, :-2]]
    result = jnp.zeros_like(field)
    for face, nb in zip(faces, neighbours):
        result = result + face[None] * (field - nb)
    return result


def velocity_solve(rhs, faces, diag):
    sigma = cheb_theta / cheb_delta
    solved = rhs / (cheb_theta * diag[None])
    change = solved
    rho_prev = 1.0 / sigma
    for step in range(DEGREE - 1):
        resid = rhs - apply_op(solved, faces)
        rho = 1.0 / (2.0 * sigma - rho_prev)
        change = rho * rho_prev * change + (2.0 * rho / cheb_delta) * resid / diag[None]
        solved = solved + change
        rho_prev = rho
    return solved


def diverge(field, owner_slot):
    col_x = jnp.sum(field[0], axis=1)
    col_z = jnp.sum(field[1], axis=1)
    below = jnp.pad(col_x[:-1], ((1, 0), (0, 0)))
    behind = jnp.pad(col_z[:, :-1], ((0, 0), (1, 0)))
    local = col_x - below + col_z - behind
    return jnp.zeros_like(local).at[:, owner_slot].set(local)


def gradient(press, owner_slot, ny):
    column = press[:, owner_slot]
    grad_x = column - jnp.pad(column[1:], ((0, 1), (0, 0)))
    grad_z = column - jnp.pad(column[:, 1:], ((0, 0), (0, 1)))
    both = jnp.stack([grad_x, grad_z])[:, :, None, :]
    return jnp.broadcast_to(both, (2, column.shape[0], ny, column.shape[1]))


def reference(forcing, viscosity, owner_slot):
    faces, diag = face_parts(viscosity)
    ny = viscosity.shape[1]
    target = diverge(velocity_solve(forcing, faces, diag), owner_slot)
    pressure = jnp.zeros_like(target)
    resid = target
    dirn = target
    rr = jnp.sum(resid * resid)
    for step in range(OUTER):
        image = diverge(velocity_solve(gradient(dirn, owner_slot, ny), faces, diag), owner_slot)
        alpha = rr / jnp.sum(dirn * image)
        pressure = pressure + alpha * dirn
        if step + 1 < OUTER:
            resid = resid - alpha * image
            fresh = jnp.sum(resid * resid)
            dirn = resid + (fresh / rr) * dirn
            rr = fresh
    velocity = velocity_solve(forcing - gradient(pressure, owner_slot, ny), faces, diag)
    return velocity, pressure
```

```python
import jax
import jax.numpy as jnp
from jax import lax
from jax.sharding import PartitionSpec as P

OUTER = 2
DEGREE = 3


cheb_theta = 1.025
cheb_delta = 0.975


def cheb_weights():
    sigma = cheb_theta / cheb_delta
    solved = [1.0 / cheb_theta] + [0.0] * (DEGREE - 1)
    change = list(solved)
    rho_prev = 1.0 / sigma
    for step in range(DEGREE - 1):
        resid = [(1.0 if k == 0 else solved[k - 1]) - solved[k] for k in range(DEGREE)]
        resid[0] = 1.0 - solved[0]
        rho = 1.0 / (2.0 * sigma - rho_prev)
        change = [rho * rho_prev * c + 2.0 * rho / cheb_delta * r for c, r in zip(change, resid)]
        solved = [s + c for s, c in zip(solved, change)]
        rho_prev = rho
    return solved


OFFSETS = [(0, 0), (1, 0), (0, 1), (2, 0), (0, 2), (1, 1), (1, -1)]


def with_halo(cells, axis, dim, width):
    count = lax.axis_size(axis)
    ends = count - 1
    head = lax.slice_in_dim(cells, 0, width, axis=dim)
    tail = lax.slice_in_dim(cells, cells.shape[dim] - width, cells.shape[dim], axis=dim)
    return jnp.concatenate(
        [
            lax.ppermute(tail, axis, [(i, i + 1) for i in range(ends)]),
            cells,
            lax.ppermute(head, axis, [(i + 1, i) for i in range(ends)]),
        ],
        axis=dim,
    )


def zs(a, s):
    if s > 0:
        return jnp.pad(a[..., s:], [(0, 0)] * (a.ndim - 1) + [(0, s)])
    return jnp.pad(a[..., :s], [(0, 0)] * (a.ndim - 1) + [(-s, 0)])


def rows(a, s):
    if s == 0:
        return a
    if s > 0:
        return jnp.pad(a[s:], ((0, s), (0, 0)))
    return jnp.pad(a[:s], ((-s, 0), (0, 0)))


def at(a, dx, dz):
    a = rows(a, dx)
    return zs(a, dz) if dz else a


def shards(forcing, viscosity, owner_slot):
    w0, w1, w2 = cheb_weights()
    slab_n, cross_n = lax.axis_size("slab"), lax.axis_size("cross")
    slab, cross = lax.axis_index("slab"), lax.axis_index("cross")
    nx, ny, nz = viscosity.shape
    v = with_halo(with_halo(viscosity, "cross", 1, 3), "slab", 0, 3)
    f = with_halo(with_halo(forcing, "cross", 2, 2), "slab", 1, 2)
    c = v[1:-1, 1:-1]
    fxp, fxm = 0.5 * (c + v[2:, 1:-1]), 0.5 * (c + v[:-2, 1:-1])
    fyp, fym = 0.5 * (c + v[1:-1, 2:]), 0.5 * (c + v[1:-1, :-2])
    fzp, fzm = 0.5 * (c + zs(c, 1)), 0.5 * (c + zs(c, -1))
    diag = fxp + fxm + fyp + fym + fzp + fzm
    xi = lax.broadcasted_iota(jnp.int32, c.shape, 0) + slab * nx - 2
    yi = lax.broadcasted_iota(jnp.int32, c.shape, 1) + cross * ny - 2
    inside = (xi >= 0) & (xi < nx * slab_n) & (yi >= 0) & (yi < ny * cross_n)
    dinv = jnp.where(inside, 1.0 / jnp.where(inside, diag, 1.0), 0.0)

    def inner(a):
        return a[..., 1:-1, 1:-1, :]

    def nbr(a, dx, dy):
        n1, n2 = a.shape[-3], a.shape[-2]
        return a[..., 1 + dx : n1 - 1 + dx, 1 + dy : n2 - 1 + dy, :]

    faces2 = (fxp, fxm, fyp, fym, fzp, fzm)
    faces1 = tuple(inner(a) for a in faces2)
    faces0 = tuple(inner(a) for a in faces1)
    d1, d0 = inner(dinv), inner(inner(dinv))

    def tapply(y, fc, di):
        fxp, fxm, fyp, fym, fzp, fzm = fc
        yc = inner(y)
        return di * (
            fxp * nbr(y, 1, 0) + fxm * nbr(y, -1, 0) + fyp * nbr(y, 0, 1)
            + fym * nbr(y, 0, -1) + fzp * zs(yc, 1) + fzm * zs(yc, -1)
        )

    y0 = dinv * f
    t1 = tapply(y0, faces1, d1)
    free = w0 * inner(inner(y0)) + tapply(w1 * inner(y0) + w2 * t1, faces0, d0)

    xp, xm, yp, ym, zp, zm = faces1
    W = {
        (0, 0): d1 * (yp * nbr(dinv, 0, 1) + ym * nbr(dinv, 0, -1)),
        (1, 0): d1 * xp * nbr(dinv, 1, 0),
        (-1, 0): d1 * xm * nbr(dinv, -1, 0),
        (0, 1): d1 * zp * zs(d1, 1),
        (0, -1): d1 * zm * zs(d1, -1),
    }
    U = {o: w2 * a for o, a in W.items()}
    U[(0, 0)] = U[(0, 0)] + w1 * d1
    xp, xm, yp, ym, zp, zm = faces0
    acc = {}

    def add(o, a):
        acc[o] = acc[o] + a if o in acc else a

    for o, a in U.items():
        ac = inner(a)
        add(o, yp * nbr(a, 0, 1) + ym * nbr(a, 0, -1))
        add((o[0] + 1, o[1]), xp * nbr(a, 1, 0))
        add((o[0] - 1, o[1]), xm * nbr(a, -1, 0))
        add((o[0], o[1] + 1), zp * zs(ac, 1))
        add((o[0], o[1] - 1), zm * zs(ac, -1))
    m = {o: d0 * a for o, a in acc.items()}
    m[(0, 0)] = m[(0, 0)] + w0 * d0

    part = jnp.stack([jnp.sum(m[o], axis=1) for o in OFFSETS] + [jnp.sum(free[0], 1), jnp.sum(free[1], 1)], 1)
    whole = lax.psum(part, "cross")
    whole = lax.all_gather(whole, "slab", axis=0, tiled=True)
    K = {o: whole[:, n] for n, o in enumerate(OFFSETS)}
    cx, cz = whole[:, 7], whole[:, 8]

    def diverge(cx, cz):
        return cx - rows(cx, -1) + cz - zs(cz, -1)

    def grad(q):
        return q - rows(q, 1), q - zs(q, 1)

    back = {o: at(a, -o[0], -o[1]) for o, a in K.items()}

    def kapply(q):
        out = K[(0, 0)] * q
        for o in OFFSETS[1:]:
            out = out + K[o] * at(q, o[0], o[1]) + back[o] * at(q, -o[0], -o[1])
        return out

    target = diverge(cx, cz)
    pressure = jnp.zeros_like(target)
    resid = dirn = target
    rr = jnp.sum(resid * resid)
    for step in range(OUTER):
        gx, gz = grad(dirn)
        image = diverge(kapply(gx), kapply(gz))
        alpha = rr / jnp.sum(dirn * image)
        pressure = pressure + alpha * dirn
        if step + 1 < OUTER:
            resid = resid - alpha * image
            fresh = jnp.sum(resid * resid)
            dirn = resid + (fresh / rr) * dirn
            rr = fresh
    g = jnp.pad(jnp.stack(grad(pressure)), ((0, 0), (2, 2), (0, 0)))
    g = lax.dynamic_slice_in_dim(g, slab * nx, nx + 4, 1)
    velocity = free
    for o, a in m.items():
        s = g[:, 2 + o[0] : 2 + o[0] + nx]
        s = zs(s, o[1]) if o[1] else s
        velocity = velocity - a[None] * s[:, :, None, :]
    mine = lax.dynamic_slice_in_dim(pressure, slab * nx, nx, 0)
    width = nz // cross_n
    cols = cross * width + jnp.arange(width, dtype=jnp.int32)
    onehot = (owner_slot[:, None] == cols[None, :]).astype(jnp.float32)
    return velocity, jnp.dot(mine, onehot, precision=lax.Precision.HIGHEST)


def solution(mesh):
    in_specs = (P(None, "slab", "cross", None), P("slab", "cross", None), P())
    out_specs = (P(None, "slab", "cross", None), P("slab", "cross"))
    return jax.shard_map(shards, mesh=mesh, in_specs=in_specs, out_specs=out_specs, check_vma=False)
```

```python
import functools

import jax
import jax.numpy as jnp
from jax import lax
from jax.experimental import pallas as pl
from jax.experimental.pallas import tpu as pltpu
from jax.sharding import PartitionSpec as P

MESH = pl.DeviceIdType.MESH

OUTER = 2
DEGREE = 3


cheb_theta = 1.025
cheb_delta = 0.975


def cheb_weights():
    sigma = cheb_theta / cheb_delta
    solved = [1.0 / cheb_theta] + [0.0] * (DEGREE - 1)
    change = list(solved)
    rho_prev = 1.0 / sigma
    for step in range(DEGREE - 1):
        resid = [(1.0 if k == 0 else solved[k - 1]) - solved[k] for k in range(DEGREE)]
        resid[0] = 1.0 - solved[0]
        rho = 1.0 / (2.0 * sigma - rho_prev)
        change = [rho * rho_prev * c + 2.0 * rho / cheb_delta * r for c, r in zip(change, resid)]
        solved = [s + c for s, c in zip(solved, change)]
        rho_prev = rho
    return solved


OFFSETS = [(0, 0), (1, 0), (0, 1), (2, 0), (0, 2), (1, 1), (1, -1)]


def moved(a, dx, dz):
    n0, n1 = a.shape
    if dx:
        row = lax.broadcasted_iota(jnp.int32, a.shape, 0)
        a = jnp.where((row + dx >= 0) & (row + dx < n0), pltpu.roll(a, (-dx) % n0, 0), 0.0)
    if dz:
        col = lax.broadcasted_iota(jnp.int32, a.shape, 1)
        a = jnp.where((col + dz >= 0) & (col + dz < n1), pltpu.roll(a, (-dz) % n1, 1), 0.0)
    return a


def cg_body(sn, cn, part, owner, gs, press, crecv, kall, kfull, back, gpad, csend, crecv_sem, ssend, srecv):
    slab, cross = lax.axis_index("slab"), lax.axis_index("cross")
    nf, nx, nz = part.shape
    barrier = pltpu.get_barrier_semaphore()
    for d in range(1, cn):
        pl.semaphore_signal(barrier, inc=1, device_id={"cross": lax.rem(cross + d, cn)}, device_id_type=MESH)
    for d in range(1, sn):
        pl.semaphore_signal(barrier, inc=1, device_id={"slab": lax.rem(slab + d, sn)}, device_id_type=MESH)
    pl.semaphore_wait(barrier, cn - 1 + sn - 1)
    copies = []
    for d in range(1, cn):
        copy = pltpu.make_async_remote_copy(
            src_ref=part, dst_ref=crecv.at[cross], send_sem=csend.at[d - 1], recv_sem=crecv_sem.at[d - 1],
            device_id={"cross": lax.rem(cross + d, cn)}, device_id_type=MESH,
        )
        copy.start()
        copies.append(copy)
    crecv[cross] = part[...]
    for copy in copies:
        copy.wait()
    for n in range(nf):
        total = crecv[0, n]
        for d in range(1, cn):
            total = total + crecv[d, n]
        kall[slab, n] = total
    copies = []
    for d in range(1, sn):
        copy = pltpu.make_async_remote_copy(
            src_ref=kall.at[slab], dst_ref=kall.at[slab], send_sem=ssend.at[d - 1], recv_sem=srecv.at[d - 1],
            device_id={"slab": lax.rem(slab + d, sn)}, device_id_type=MESH,
        )
        copy.start()
        copies.append(copy)
    for copy in copies:
        copy.wait()
    for n in range(nf):
        for s in range(sn):
            kfull[n, s * nx : (s + 1) * nx, :] = kall[s, n]
    for n, o in enumerate(OFFSETS[1:]):
        back[n] = moved(kfull[n + 1], -o[0], -o[1])

    def diverge(cx, cz):
        return cx - moved(cx, -1, 0) + cz - moved(cz, 0, -1)

    def kapply(q):
        out = kfull[0] * q
        for n, o in enumerate(OFFSETS[1:]):
            out = out + kfull[n + 1] * moved(q, o[0], o[1]) + back[n] * moved(q, -o[0], -o[1])
        return out

    def grad(q):
        return q - moved(q, 1, 0), q - moved(q, 0, 1)

    target = diverge(kfull[nf - 2], kfull[nf - 1])
    pressure = jnp.zeros_like(target)
    resid = dirn = target
    rr = jnp.sum(resid * resid)
    for step in range(OUTER):
        gx, gz = grad(dirn)
        image = diverge(kapply(gx), kapply(gz))
        alpha = rr / jnp.sum(dirn * image)
        pressure = pressure + alpha * dirn
        if step + 1 < OUTER:
            resid = resid - alpha * image
            fresh = jnp.sum(resid * resid)
            dirn = resid + (fresh / rr) * dirn
            rr = fresh
    zero = jnp.zeros((8, nz), jnp.float32)
    full = sn * nx
    for c, q in enumerate(grad(pressure)):
        for dz in range(-2, 3):
            gpad[dz + 2, c, 0:8, :] = zero
            gpad[dz + 2, c, full + 8 : full + 16, :] = zero
            gpad[dz + 2, c, 8 : full + 8, :] = moved(q, 0, dz)
    kfull[0] = pressure
    width = press.shape[1]
    slot = lax.broadcasted_iota(jnp.int32, (width, nz), 0) + cross * width
    onehot = (jnp.broadcast_to(owner[...], (width, nz)) == slot).astype(jnp.float32)
    for s in range(sn):

        @pl.when(slab == s)
        def _():
            gs[...] = gpad[:, :, 6 + s * nx : 10 + (s + 1) * nx, :]
            press[...] = lax.dot_general(
                kfull[0, s * nx : (s + 1) * nx, :], onehot, (((1,), (1,)), ((), ())),
                precision=lax.Precision.HIGHEST, preferred_element_type=jnp.float32,
            )


def column_cg(part, owner, sn, cn):
    nf, nx, nz = part.shape
    f32 = jnp.float32
    vmem = pl.BlockSpec(memory_space=pltpu.VMEM)
    return pl.pallas_call(
        functools.partial(cg_body, sn, cn),
        out_shape=(
            jax.ShapeDtypeStruct((5, 2, nx + 4, nz), f32),
            jax.ShapeDtypeStruct((nx, nz // cn), f32),
        ),
        in_specs=[vmem, vmem],
        out_specs=(vmem, vmem),
        scratch_shapes=[
            pltpu.VMEM((cn, nf, nx, nz), f32),
            pltpu.VMEM((sn, nf, nx, nz), f32),
            pltpu.VMEM((nf, sn * nx, nz), f32),
            pltpu.VMEM((nf - 3, sn * nx, nz), f32),
            pltpu.VMEM((5, 2, sn * nx + 16, nz), f32),
            pltpu.SemaphoreType.DMA((cn - 1,)),
            pltpu.SemaphoreType.DMA((cn - 1,)),
            pltpu.SemaphoreType.DMA((sn - 1,)),
            pltpu.SemaphoreType.DMA((sn - 1,)),
        ],
        compiler_params=pltpu.CompilerParams(collective_id=0, has_side_effects=True),
        name="column_cg",
    )(part, owner)


def with_halo(cells, axis, dim, width):
    count = lax.axis_size(axis)
    ends = count - 1
    head = lax.slice_in_dim(cells, 0, width, axis=dim)
    tail = lax.slice_in_dim(cells, cells.shape[dim] - width, cells.shape[dim], axis=dim)
    return jnp.concatenate(
        [
            lax.ppermute(tail, axis, [(i, i + 1) for i in range(ends)]),
            cells,
            lax.ppermute(head, axis, [(i + 1, i) for i in range(ends)]),
        ],
        axis=dim,
    )


def zs(a, s):
    if s > 0:
        return jnp.pad(a[..., s:], [(0, 0)] * (a.ndim - 1) + [(0, s)])
    return jnp.pad(a[..., :s], [(0, 0)] * (a.ndim - 1) + [(-s, 0)])


def shards(forcing, viscosity, owner_slot):
    w0, w1, w2 = cheb_weights()
    slab_n, cross_n = lax.axis_size("slab"), lax.axis_size("cross")
    slab, cross = lax.axis_index("slab"), lax.axis_index("cross")
    nx, ny, nz = viscosity.shape
    v = with_halo(with_halo(viscosity, "cross", 1, 3), "slab", 0, 3)
    f = with_halo(with_halo(forcing, "cross", 2, 2), "slab", 1, 2)
    c = v[1:-1, 1:-1]
    fxp, fxm = 0.5 * (c + v[2:, 1:-1]), 0.5 * (c + v[:-2, 1:-1])
    fyp, fym = 0.5 * (c + v[1:-1, 2:]), 0.5 * (c + v[1:-1, :-2])
    fzp, fzm = 0.5 * (c + zs(c, 1)), 0.5 * (c + zs(c, -1))
    diag = fxp + fxm + fyp + fym + fzp + fzm
    xi = lax.broadcasted_iota(jnp.int32, c.shape, 0) + slab * nx - 2
    yi = lax.broadcasted_iota(jnp.int32, c.shape, 1) + cross * ny - 2
    inside = (xi >= 0) & (xi < nx * slab_n) & (yi >= 0) & (yi < ny * cross_n)
    dinv = jnp.where(inside, 1.0 / jnp.where(inside, diag, 1.0), 0.0)

    def inner(a):
        return a[..., 1:-1, 1:-1, :]

    def nbr(a, dx, dy):
        n1, n2 = a.shape[-3], a.shape[-2]
        return a[..., 1 + dx : n1 - 1 + dx, 1 + dy : n2 - 1 + dy, :]

    faces2 = (fxp, fxm, fyp, fym, fzp, fzm)
    faces1 = tuple(inner(a) for a in faces2)
    faces0 = tuple(inner(a) for a in faces1)
    d1, d0 = inner(dinv), inner(inner(dinv))

    def tapply(y, fc, di):
        fxp, fxm, fyp, fym, fzp, fzm = fc
        yc = inner(y)
        return di * (
            fxp * nbr(y, 1, 0) + fxm * nbr(y, -1, 0) + fyp * nbr(y, 0, 1)
            + fym * nbr(y, 0, -1) + fzp * zs(yc, 1) + fzm * zs(yc, -1)
        )

    y0 = dinv * f
    t1 = tapply(y0, faces1, d1)
    free = w0 * inner(inner(y0)) + tapply(w1 * inner(y0) + w2 * t1, faces0, d0)

    xp, xm, yp, ym, zp, zm = faces1
    W = {
        (0, 0): d1 * (yp * nbr(dinv, 0, 1) + ym * nbr(dinv, 0, -1)),
        (1, 0): d1 * xp * nbr(dinv, 1, 0),
        (-1, 0): d1 * xm * nbr(dinv, -1, 0),
        (0, 1): d1 * zp * zs(d1, 1),
        (0, -1): d1 * zm * zs(d1, -1),
    }
    U = {o: w2 * a for o, a in W.items()}
    U[(0, 0)] = U[(0, 0)] + w1 * d1
    xp, xm, yp, ym, zp, zm = faces0
    acc = {}

    def add(o, a):
        acc[o] = acc[o] + a if o in acc else a

    for o, a in U.items():
        ac = inner(a)
        add(o, yp * nbr(a, 0, 1) + ym * nbr(a, 0, -1))
        add((o[0] + 1, o[1]), xp * nbr(a, 1, 0))
        add((o[0] - 1, o[1]), xm * nbr(a, -1, 0))
        add((o[0], o[1] + 1), zp * zs(ac, 1))
        add((o[0], o[1] - 1), zm * zs(ac, -1))
    m = {o: d0 * a for o, a in acc.items()}
    m[(0, 0)] = m[(0, 0)] + w0 * d0

    part = jnp.stack([jnp.sum(m[o], axis=1) for o in OFFSETS] + [jnp.sum(free[0], 1), jnp.sum(free[1], 1)], 0)
    gs, pressure = column_cg(part, owner_slot.reshape(1, nz), slab_n, cross_n)
    velocity = free
    for o, a in m.items():
        s = gs[2 + o[1], :, 2 + o[0] : 2 + o[0] + nx]
        velocity = velocity - a[None] * s[:, :, None, :]
    return velocity, pressure


def solution(mesh):
    in_specs = (P(None, "slab", "cross", None), P("slab", "cross", None), P())
    out_specs = (P(None, "slab", "cross", None), P("slab", "cross"))
    return jax.shard_map(shards, mesh=mesh, in_specs=in_specs, out_specs=out_specs, check_vma=False)
```

```python
import functools

import jax
import jax.numpy as jnp
from jax import lax
from jax.experimental import pallas as pl
from jax.experimental.pallas import tpu as pltpu
from jax.sharding import PartitionSpec as P

MESH = pl.DeviceIdType.MESH

OUTER = 2
DEGREE = 3


cheb_theta = 1.025
cheb_delta = 0.975


def cheb_weights():
    sigma = cheb_theta / cheb_delta
    solved = [1.0 / cheb_theta] + [0.0] * (DEGREE - 1)
    change = list(solved)
    rho_prev = 1.0 / sigma
    for step in range(DEGREE - 1):
        resid = [(1.0 if k == 0 else solved[k - 1]) - solved[k] for k in range(DEGREE)]
        resid[0] = 1.0 - solved[0]
        rho = 1.0 / (2.0 * sigma - rho_prev)
        change = [rho * rho_prev * c + 2.0 * rho / cheb_delta * r for c, r in zip(change, resid)]
        solved = [s + c for s, c in zip(solved, change)]
        rho_prev = rho
    return solved


OFFSETS = [(0, 0), (1, 0), (0, 1), (2, 0), (0, 2), (1, 1), (1, -1)]


def moved(a, dx, dz):
    n0, n1 = a.shape
    if dx:
        row = lax.broadcasted_iota(jnp.int32, a.shape, 0)
        a = jnp.where((row + dx >= 0) & (row + dx < n0), pltpu.roll(a, (-dx) % n0, 0), 0.0)
    if dz:
        col = lax.broadcasted_iota(jnp.int32, a.shape, 1)
        a = jnp.where((col + dz >= 0) & (col + dz < n1), pltpu.roll(a, (-dz) % n1, 1), 0.0)
    return a


def cg_body(sn, cn, part, owner, gs, press, crecv, kall, kfull, back, gpad, csend, crecv_sem, ssend, srecv):
    slab, cross = lax.axis_index("slab"), lax.axis_index("cross")
    nf, nx, nz = part.shape
    barrier = pltpu.get_barrier_semaphore()
    for d in range(1, cn):
        pl.semaphore_signal(barrier, inc=1, device_id={"cross": lax.rem(cross + d, cn)}, device_id_type=MESH)
    zn = sn // 2
    place, core = slab // 2, lax.rem(slab, 2)
    for d in range(1, zn):
        pl.semaphore_signal(
            barrier, inc=1, device_id={"slab": lax.rem(place + d, zn) * 2 + core}, device_id_type=MESH
        )
    partner = place * 2 + 1 - core
    pl.semaphore_signal(barrier, inc=1, device_id={"slab": partner}, device_id_type=MESH)
    pl.semaphore_wait(barrier, cn - 1 + zn)
    copies = []
    for d in range(1, cn):
        copy = pltpu.make_async_remote_copy(
            src_ref=part, dst_ref=crecv.at[cross], send_sem=csend.at[d - 1], recv_sem=crecv_sem.at[d - 1],
            device_id={"cross": lax.rem(cross + d, cn)}, device_id_type=MESH,
        )
        copy.start()
        copies.append(copy)
    crecv[cross] = part[...]
    for copy in copies:
        copy.wait()
    for n in range(nf):
        total = crecv[0, n]
        for d in range(1, cn):
            total = total + crecv[d, n]
        kall[slab, n] = total
    def pass_on(block, target, sem):
        copy = pltpu.make_async_remote_copy(
            src_ref=kall.at[block], dst_ref=kall.at[block], send_sem=ssend.at[sem], recv_sem=srecv.at[sem],
            device_id={"slab": target}, device_id_type=MESH,
        )
        copy.start()
        return copy

    far = [pass_on(slab, lax.rem(place + d, zn) * 2 + core, d - 1) for d in range(1, zn)]
    near = [pass_on(slab, partner, zn - 1)]
    for d in range(1, zn):
        far[d - 1].wait_recv()
        near.append(pass_on(lax.rem(place - d + zn, zn) * 2 + core, partner, zn - 1 + d))
    for copy in near:
        copy.wait()
    for copy in far:
        copy.wait_send()
    for n in range(nf):
        for s in range(sn):
            kfull[n, s * nx : (s + 1) * nx, :] = kall[s, n]
    for n, o in enumerate(OFFSETS[1:]):
        back[n] = moved(kfull[n + 1], -o[0], -o[1])

    def diverge(cx, cz):
        return cx - moved(cx, -1, 0) + cz - moved(cz, 0, -1)

    def kapply(q):
        out = kfull[0] * q
        for n, o in enumerate(OFFSETS[1:]):
            out = out + kfull[n + 1] * moved(q, o[0], o[1]) + back[n] * moved(q, -o[0], -o[1])
        return out

    def grad(q):
        return q - moved(q, 1, 0), q - moved(q, 0, 1)

    target = diverge(kfull[nf - 2], kfull[nf - 1])
    pressure = jnp.zeros_like(target)
    resid = dirn = target
    rr = jnp.sum(resid * resid)
    for step in range(OUTER):
        gx, gz = grad(dirn)
        image = diverge(kapply(gx), kapply(gz))
        alpha = rr / jnp.sum(dirn * image)
        pressure = pressure + alpha * dirn
        if step + 1 < OUTER:
            resid = resid - alpha * image
            fresh = jnp.sum(resid * resid)
            dirn = resid + (fresh / rr) * dirn
            rr = fresh
    zero = jnp.zeros((8, nz), jnp.float32)
    full = sn * nx
    for c, q in enumerate(grad(pressure)):
        for dz in range(-2, 3):
            gpad[dz + 2, c, 0:8, :] = zero
            gpad[dz + 2, c, full + 8 : full + 16, :] = zero
            gpad[dz + 2, c, 8 : full + 8, :] = moved(q, 0, dz)
    kfull[0] = pressure
    width = press.shape[1]
    slot = lax.broadcasted_iota(jnp.int32, (width, nz), 0) + cross * width
    onehot = (jnp.broadcast_to(owner[...], (width, nz)) == slot).astype(jnp.float32)
    for s in range(sn):

        @pl.when(slab == s)
        def _():
            gs[...] = gpad[:, :, 6 + s * nx : 10 + (s + 1) * nx, :]
            press[...] = lax.dot_general(
                kfull[0, s * nx : (s + 1) * nx, :], onehot, (((1,), (1,)), ((), ())),
                precision=lax.Precision.HIGHEST, preferred_element_type=jnp.float32,
            )


def column_cg(part, owner, sn, cn):
    nf, nx, nz = part.shape
    f32 = jnp.float32
    vmem = pl.BlockSpec(memory_space=pltpu.VMEM)
    return pl.pallas_call(
        functools.partial(cg_body, sn, cn),
        out_shape=(
            jax.ShapeDtypeStruct((5, 2, nx + 4, nz), f32),
            jax.ShapeDtypeStruct((nx, nz // cn), f32),
        ),
        in_specs=[vmem, vmem],
        out_specs=(vmem, vmem),
        scratch_shapes=[
            pltpu.VMEM((cn, nf, nx, nz), f32),
            pltpu.VMEM((sn, nf, nx, nz), f32),
            pltpu.VMEM((nf, sn * nx, nz), f32),
            pltpu.VMEM((nf - 3, sn * nx, nz), f32),
            pltpu.VMEM((5, 2, sn * nx + 16, nz), f32),
            pltpu.SemaphoreType.DMA((cn - 1,)),
            pltpu.SemaphoreType.DMA((cn - 1,)),
            pltpu.SemaphoreType.DMA((sn - 1,)),
            pltpu.SemaphoreType.DMA((sn - 1,)),
        ],
        compiler_params=pltpu.CompilerParams(collective_id=0, has_side_effects=True),
        name="column_cg",
    )(part, owner)


def halo_body(sn, cn, visc, forc, ypack, vx, fx, yp, cp, send, recv):
    slab, cross = lax.axis_index("slab"), lax.axis_index("cross")
    nx = visc.shape[0]
    sides = (("slab", slab - 1, slab > 0), ("slab", slab + 1, slab < sn - 1))
    walls = (("cross", cross - 1, cross > 0), ("cross", cross + 1, cross < cn - 1))
    barrier = pltpu.get_barrier_semaphore()
    for axis, peer, there in sides + walls:

        @pl.when(there)
        def _():
            pl.semaphore_signal(barrier, inc=1, device_id={axis: peer}, device_id_type=MESH)

    around = [jnp.where(there, 1, 0) for axis, peer, there in sides + walls]
    pl.semaphore_wait(barrier, around[0] + around[1] + around[2] + around[3])

    def x_copies(s):
        axis, peer, there = sides[s]
        v0, f0 = (0, 0) if s == 0 else (nx - 3, nx - 2)
        pairs = ((visc.at[pl.ds(v0, 3)], vx.at[1 - s]), (forc.at[:, pl.ds(f0, 2)], fx.at[1 - s]))
        return [
            pltpu.make_async_remote_copy(
                src_ref=a, dst_ref=b, send_sem=send.at[2 * s + n], recv_sem=recv.at[2 * (1 - s) + n],
                device_id={axis: peer}, device_id_type=MESH,
            )
            for n, (a, b) in enumerate(pairs)
        ]

    def y_copy(w):
        axis, peer, there = walls[w]
        return pltpu.make_async_remote_copy(
            src_ref=ypack.at[w], dst_ref=yp.at[1 - w], send_sem=send.at[4 + w], recv_sem=recv.at[4 + 1 - w],
            device_id={axis: peer}, device_id_type=MESH,
        )

    def corner_copy(w, s):
        axis, peer, there = sides[s]
        return pltpu.make_async_remote_copy(
            src_ref=yp.at[w], dst_ref=cp.at[1 - s, w], send_sem=send.at[6 + 2 * w + s],
            recv_sem=recv.at[6 + 2 * w + 1 - s], device_id={axis: peer}, device_id_type=MESH,
        )

    def y_in(w):
        return pltpu.make_async_remote_copy(
            src_ref=ypack.at[w], dst_ref=yp.at[w], send_sem=send.at[4 + w], recv_sem=recv.at[4 + w],
            device_id={"cross": walls[w][1]}, device_id_type=MESH,
        )

    def corner_in(w, s):
        return pltpu.make_async_remote_copy(
            src_ref=yp.at[w], dst_ref=cp.at[s, w], send_sem=send.at[6 + 2 * w + s],
            recv_sem=recv.at[6 + 2 * w + s], device_id={"slab": sides[s][1]}, device_id_type=MESH,
        )

    def x_in(s):
        pairs = ((visc.at[pl.ds(0, 3)], vx.at[s]), (forc.at[:, pl.ds(0, 2)], fx.at[s]))
        return [
            pltpu.make_async_remote_copy(
                src_ref=a, dst_ref=b, send_sem=send.at[2 * s + n], recv_sem=recv.at[2 * s + n],
                device_id={"slab": sides[s][1]}, device_id_type=MESH,
            )
            for n, (a, b) in enumerate(pairs)
        ]

    for w in range(2):

        @pl.when(walls[w][2])
        def _():
            y_copy(w).start()

    for s in range(2):

        @pl.when(sides[s][2])
        def _():
            for copy in x_copies(s):
                copy.start()

    for w in range(2):

        @pl.when(walls[w][2])
        def _():
            y_in(w).wait_recv()
            for s in range(2):

                @pl.when(sides[s][2])
                def _():
                    corner_copy(w, s).start()

    for s in range(2):

        @pl.when(sides[s][2])
        def _():
            for copy in x_in(s):
                copy.wait_recv()
            for copy in x_copies(s):
                copy.wait_send()

    for w in range(2):

        @pl.when(walls[w][2])
        def _():
            y_copy(w).wait_send()
            for s in range(2):

                @pl.when(sides[s][2])
                def _():
                    corner_in(w, s).wait_recv()
                    corner_copy(w, s).wait_send()


def halos(viscosity, forcing, sn, cn):
    nx, ny, nz = viscosity.shape
    f32 = jnp.float32

    def packed(v0, f0):
        a = viscosity[:, v0 : v0 + 3].reshape(3 * nx, nz)
        b = forcing[:, :, f0 : f0 + 2].reshape(4 * nx, nz)
        return jnp.concatenate([a, b], 0)

    ypack = jnp.stack([packed(0, 0), packed(ny - 3, ny - 2)])
    anywhere = pl.BlockSpec(memory_space=pl.ANY)
    vx, fx, yp, cp = pl.pallas_call(
        functools.partial(halo_body, sn, cn),
        out_shape=(
            jax.ShapeDtypeStruct((2, 3, ny, nz), f32),
            jax.ShapeDtypeStruct((2, 2, 2, ny, nz), f32),
            jax.ShapeDtypeStruct((2, 7 * nx, nz), f32),
            jax.ShapeDtypeStruct((2, 2, 7 * nx, nz), f32),
        ),
        in_specs=[anywhere] * 3,
        out_specs=(anywhere,) * 4,
        scratch_shapes=[pltpu.SemaphoreType.DMA((10,)), pltpu.SemaphoreType.DMA((10,))],
        compiler_params=pltpu.CompilerParams(collective_id=1, has_side_effects=True),
        name="halos",
    )(viscosity, forcing, ypack)
    slab, cross = lax.axis_index("slab"), lax.axis_index("cross")
    side = (slab > 0, slab < sn - 1)
    wall = (cross > 0, cross < cn - 1)

    def only(cond, a):
        return jnp.where(cond, a, 0.0)

    def unpacked(p):
        return p[: 3 * nx].reshape(nx, 3, nz), p[3 * nx :].reshape(2, nx, 2, nz)

    yv, yf = zip(*[unpacked(only(wall[w], yp[w])) for w in range(2)])
    vs, fs = [jnp.concatenate([yv[0], viscosity, yv[1]], 1)], [jnp.concatenate([yf[0], forcing, yf[1]], 2)]
    for s in range(2):
        cv, cf = zip(*[unpacked(only(side[s] & wall[w], cp[s, w])) for w in range(2)])
        vcut, fcut = ((nx - 3, nx), (nx - 2, nx)) if s == 0 else ((0, 3), (0, 2))
        cv = [a[vcut[0] : vcut[1]] for a in cv]
        cf = [a[:, fcut[0] : fcut[1]] for a in cf]
        vs.append(jnp.concatenate([cv[0], only(side[s], vx[s]), cv[1]], 1))
        fs.append(jnp.concatenate([cf[0], only(side[s], fx[s]), cf[1]], 2))
    return jnp.concatenate([vs[1], vs[0], vs[2]], 0), jnp.concatenate([fs[1], fs[0], fs[2]], 1)


def zs(a, s):
    if s > 0:
        return jnp.pad(a[..., s:], [(0, 0)] * (a.ndim - 1) + [(0, s)])
    return jnp.pad(a[..., :s], [(0, 0)] * (a.ndim - 1) + [(-s, 0)])


def shards(forcing, viscosity, owner_slot):
    w0, w1, w2 = cheb_weights()
    slab_n, cross_n = lax.axis_size("slab"), lax.axis_size("cross")
    slab, cross = lax.axis_index("slab"), lax.axis_index("cross")
    nx, ny, nz = viscosity.shape
    v, f = halos(viscosity, forcing, slab_n, cross_n)
    c = v[1:-1, 1:-1]
    fxp, fxm = 0.5 * (c + v[2:, 1:-1]), 0.5 * (c + v[:-2, 1:-1])
    fyp, fym = 0.5 * (c + v[1:-1, 2:]), 0.5 * (c + v[1:-1, :-2])
    fzp, fzm = 0.5 * (c + zs(c, 1)), 0.5 * (c + zs(c, -1))
    diag = fxp + fxm + fyp + fym + fzp + fzm
    xi = lax.broadcasted_iota(jnp.int32, c.shape, 0) + slab * nx - 2
    yi = lax.broadcasted_iota(jnp.int32, c.shape, 1) + cross * ny - 2
    inside = (xi >= 0) & (xi < nx * slab_n) & (yi >= 0) & (yi < ny * cross_n)
    dinv = jnp.where(inside, 1.0 / jnp.where(inside, diag, 1.0), 0.0)

    def inner(a):
        return a[..., 1:-1, 1:-1, :]

    def nbr(a, dx, dy):
        n1, n2 = a.shape[-3], a.shape[-2]
        return a[..., 1 + dx : n1 - 1 + dx, 1 + dy : n2 - 1 + dy, :]

    faces2 = (fxp, fxm, fyp, fym, fzp, fzm)
    faces1 = tuple(inner(a) for a in faces2)
    faces0 = tuple(inner(a) for a in faces1)
    d1, d0 = inner(dinv), inner(inner(dinv))

    def tapply(y, fc, di):
        fxp, fxm, fyp, fym, fzp, fzm = fc
        yc = inner(y)
        return di * (
            fxp * nbr(y, 1, 0) + fxm * nbr(y, -1, 0) + fyp * nbr(y, 0, 1)
            + fym * nbr(y, 0, -1) + fzp * zs(yc, 1) + fzm * zs(yc, -1)
        )

    y0 = dinv * f
    t1 = tapply(y0, faces1, d1)
    free = w0 * inner(inner(y0)) + tapply(w1 * inner(y0) + w2 * t1, faces0, d0)

    xp, xm, yp, ym, zp, zm = faces1
    W = {
        (0, 0): d1 * (yp * nbr(dinv, 0, 1) + ym * nbr(dinv, 0, -1)),
        (1, 0): d1 * xp * nbr(dinv, 1, 0),
        (-1, 0): d1 * xm * nbr(dinv, -1, 0),
        (0, 1): d1 * zp * zs(d1, 1),
        (0, -1): d1 * zm * zs(d1, -1),
    }
    U = {o: w2 * a for o, a in W.items()}
    U[(0, 0)] = U[(0, 0)] + w1 * d1
    xp, xm, yp, ym, zp, zm = faces0
    acc = {}

    def add(o, a):
        acc[o] = acc[o] + a if o in acc else a

    for o, a in U.items():
        ac = inner(a)
        add(o, yp * nbr(a, 0, 1) + ym * nbr(a, 0, -1))
        add((o[0] + 1, o[1]), xp * nbr(a, 1, 0))
        add((o[0] - 1, o[1]), xm * nbr(a, -1, 0))
        add((o[0], o[1] + 1), zp * zs(ac, 1))
        add((o[0], o[1] - 1), zm * zs(ac, -1))
    m = {o: d0 * a for o, a in acc.items()}
    m[(0, 0)] = m[(0, 0)] + w0 * d0

    part = jnp.stack([jnp.sum(m[o], axis=1) for o in OFFSETS] + [jnp.sum(free[0], 1), jnp.sum(free[1], 1)], 0)
    gs, pressure = column_cg(part, owner_slot.reshape(1, nz), slab_n, cross_n)
    velocity = free
    for o, a in m.items():
        s = gs[2 + o[1], :, 2 + o[0] : 2 + o[0] + nx]
        velocity = velocity - a[None] * s[:, :, None, :]
    return velocity, pressure


def solution(mesh):
    in_specs = (P(None, "slab", "cross", None), P("slab", "cross", None), P())
    out_specs = (P(None, "slab", "cross", None), P("slab", "cross"))
    return jax.shard_map(shards, mesh=mesh, in_specs=in_specs, out_specs=out_specs, check_vma=False)
```

```python
import functools

import jax
import jax.numpy as jnp
from jax import lax
from jax.experimental import pallas as pl
from jax.experimental.pallas import tpu as pltpu
from jax.sharding import PartitionSpec as P

MESH = pl.DeviceIdType.MESH

OUTER = 2
DEGREE = 3


cheb_theta = 1.025
cheb_delta = 0.975


def cheb_weights():
    sigma = cheb_theta / cheb_delta
    solved = [1.0 / cheb_theta] + [0.0] * (DEGREE - 1)
    change = list(solved)
    rho_prev = 1.0 / sigma
    for step in range(DEGREE - 1):
        resid = [(1.0 if k == 0 else solved[k - 1]) - solved[k] for k in range(DEGREE)]
        resid[0] = 1.0 - solved[0]
        rho = 1.0 / (2.0 * sigma - rho_prev)
        change = [rho * rho_prev * c + 2.0 * rho / cheb_delta * r for c, r in zip(change, resid)]
        solved = [s + c for s, c in zip(solved, change)]
        rho_prev = rho
    return solved


OFFSETS = [(0, 0), (1, 0), (0, 1), (2, 0), (0, 2), (1, 1), (1, -1)]


def moved(a, dx, dz):
    n0, n1 = a.shape
    if dx:
        row = lax.broadcasted_iota(jnp.int32, a.shape, 0)
        a = jnp.where((row + dx >= 0) & (row + dx < n0), pltpu.roll(a, (-dx) % n0, 0), 0.0)
    if dz:
        col = lax.broadcasted_iota(jnp.int32, a.shape, 1)
        a = jnp.where((col + dz >= 0) & (col + dz < n1), pltpu.roll(a, (-dz) % n1, 1), 0.0)
    return a


def cg_body(sn, cn, part, owner, gs, press, crecv, kall, kfull, back, gpad, csend, crecv_sem, ssend, srecv):
    slab, cross = lax.axis_index("slab"), lax.axis_index("cross")
    nf, nx, nz = part.shape
    barrier = pltpu.get_barrier_semaphore()
    for d in range(1, cn):
        pl.semaphore_signal(barrier, inc=1, device_id={"cross": lax.rem(cross + d, cn)}, device_id_type=MESH)
    zn = sn // 2
    place, core = slab // 2, lax.rem(slab, 2)
    for d in range(1, zn):
        pl.semaphore_signal(
            barrier, inc=1, device_id={"slab": lax.rem(place + d, zn) * 2 + core}, device_id_type=MESH
        )
    partner = place * 2 + 1 - core
    pl.semaphore_signal(barrier, inc=1, device_id={"slab": partner}, device_id_type=MESH)
    pl.semaphore_wait(barrier, cn - 1 + zn)
    copies = []
    for d in range(1, cn):
        copy = pltpu.make_async_remote_copy(
            src_ref=part, dst_ref=crecv.at[cross], send_sem=csend.at[d - 1], recv_sem=crecv_sem.at[d - 1],
            device_id={"cross": lax.rem(cross + d, cn)}, device_id_type=MESH,
        )
        copy.start()
        copies.append(copy)
    crecv[cross] = part[...]
    for copy in copies:
        copy.wait()
    for n in range(nf):
        total = crecv[0, n]
        for d in range(1, cn):
            total = total + crecv[d, n]
        kall[slab, n] = total
    def pass_on(block, target, sem):
        copy = pltpu.make_async_remote_copy(
            src_ref=kall.at[block], dst_ref=kall.at[block], send_sem=ssend.at[sem], recv_sem=srecv.at[sem],
            device_id={"slab": target}, device_id_type=MESH,
        )
        copy.start()
        return copy

    far = [pass_on(slab, lax.rem(place + d, zn) * 2 + core, d - 1) for d in range(1, zn)]
    near = [pass_on(slab, partner, zn - 1)]
    for d in range(1, zn):
        far[d - 1].wait_recv()
        near.append(pass_on(lax.rem(place - d + zn, zn) * 2 + core, partner, zn - 1 + d))
    for copy in near:
        copy.wait()
    for copy in far:
        copy.wait_send()
    for n in range(nf):
        for s in range(sn):
            kfull[n, s * nx : (s + 1) * nx, :] = kall[s, n]
    for n, o in enumerate(OFFSETS[1:]):
        back[n] = moved(kfull[n + 1], -o[0], -o[1])

    def diverge(cx, cz):
        return cx - moved(cx, -1, 0) + cz - moved(cz, 0, -1)

    def kapply(q):
        out = kfull[0] * q
        for n, o in enumerate(OFFSETS[1:]):
            out = out + kfull[n + 1] * moved(q, o[0], o[1]) + back[n] * moved(q, -o[0], -o[1])
        return out

    def grad(q):
        return q - moved(q, 1, 0), q - moved(q, 0, 1)

    target = diverge(kfull[nf - 2], kfull[nf - 1])
    pressure = jnp.zeros_like(target)
    resid = dirn = target
    rr = jnp.sum(resid * resid)
    for step in range(OUTER):
        gx, gz = grad(dirn)
        image = diverge(kapply(gx), kapply(gz))
        alpha = rr / jnp.sum(dirn * image)
        pressure = pressure + alpha * dirn
        if step + 1 < OUTER:
            resid = resid - alpha * image
            fresh = jnp.sum(resid * resid)
            dirn = resid + (fresh / rr) * dirn
            rr = fresh
    zero = jnp.zeros((8, nz), jnp.float32)
    full = sn * nx
    for c, q in enumerate(grad(pressure)):
        for dz in range(-2, 3):
            gpad[dz + 2, c, 0:8, :] = zero
            gpad[dz + 2, c, full + 8 : full + 16, :] = zero
            gpad[dz + 2, c, 8 : full + 8, :] = moved(q, 0, dz)
    kfull[0] = pressure
    width = press.shape[1]
    slot = lax.broadcasted_iota(jnp.int32, (width, nz), 0) + cross * width
    onehot = (jnp.broadcast_to(owner[...], (width, nz)) == slot).astype(jnp.float32)
    for s in range(sn):

        @pl.when(slab == s)
        def _():
            gs[...] = gpad[:, :, 6 + s * nx : 10 + (s + 1) * nx, :]
            press[...] = lax.dot_general(
                kfull[0, s * nx : (s + 1) * nx, :], onehot, (((1,), (1,)), ((), ())),
                precision=lax.Precision.HIGHEST, preferred_element_type=jnp.float32,
            )


def column_cg(part, owner, sn, cn):
    nf, nx, nz = part.shape
    f32 = jnp.float32
    vmem = pl.BlockSpec(memory_space=pltpu.VMEM)
    return pl.pallas_call(
        functools.partial(cg_body, sn, cn),
        out_shape=(
            jax.ShapeDtypeStruct((5, 2, nx + 4, nz), f32),
            jax.ShapeDtypeStruct((nx, nz // cn), f32),
        ),
        in_specs=[vmem, vmem],
        out_specs=(vmem, vmem),
        scratch_shapes=[
            pltpu.VMEM((cn, nf, nx, nz), f32),
            pltpu.VMEM((sn, nf, nx, nz), f32),
            pltpu.VMEM((nf, sn * nx, nz), f32),
            pltpu.VMEM((nf - 3, sn * nx, nz), f32),
            pltpu.VMEM((5, 2, sn * nx + 16, nz), f32),
            pltpu.SemaphoreType.DMA((cn - 1,)),
            pltpu.SemaphoreType.DMA((cn - 1,)),
            pltpu.SemaphoreType.DMA((sn - 1,)),
            pltpu.SemaphoreType.DMA((sn - 1,)),
        ],
        compiler_params=pltpu.CompilerParams(collective_id=0, has_side_effects=True),
        name="column_cg",
    )(part, owner)


def halo_body(sn, cn, visc, forc, ypack, vx, fx, yp, cp, send, recv):
    slab, cross = lax.axis_index("slab"), lax.axis_index("cross")
    nx = visc.shape[0]
    sides = (("slab", slab - 1, slab > 0), ("slab", slab + 1, slab < sn - 1))
    walls = (("cross", cross - 1, cross > 0), ("cross", cross + 1, cross < cn - 1))
    barrier = pltpu.get_barrier_semaphore()
    for axis, peer, there in sides + walls:

        @pl.when(there)
        def _():
            pl.semaphore_signal(barrier, inc=1, device_id={axis: peer}, device_id_type=MESH)

    around = [jnp.where(there, 1, 0) for axis, peer, there in sides + walls]
    pl.semaphore_wait(barrier, around[0] + around[1] + around[2] + around[3])

    def x_copies(s):
        axis, peer, there = sides[s]
        v0, f0 = (0, 0) if s == 0 else (nx - 3, nx - 2)
        pairs = ((visc.at[pl.ds(v0, 3)], vx.at[1 - s]), (forc.at[:, pl.ds(f0, 2)], fx.at[1 - s]))
        return [
            pltpu.make_async_remote_copy(
                src_ref=a, dst_ref=b, send_sem=send.at[2 * s + n], recv_sem=recv.at[2 * (1 - s) + n],
                device_id={axis: peer}, device_id_type=MESH,
            )
            for n, (a, b) in enumerate(pairs)
        ]

    def y_copy(w):
        axis, peer, there = walls[w]
        return pltpu.make_async_remote_copy(
            src_ref=ypack.at[w], dst_ref=yp.at[1 - w], send_sem=send.at[4 + w], recv_sem=recv.at[4 + 1 - w],
            device_id={axis: peer}, device_id_type=MESH,
        )

    def corner_copy(w, s):
        axis, peer, there = sides[s]
        return pltpu.make_async_remote_copy(
            src_ref=yp.at[w], dst_ref=cp.at[1 - s, w], send_sem=send.at[6 + 2 * w + s],
            recv_sem=recv.at[6 + 2 * w + 1 - s], device_id={axis: peer}, device_id_type=MESH,
        )

    def y_in(w):
        return pltpu.make_async_remote_copy(
            src_ref=ypack.at[w], dst_ref=yp.at[w], send_sem=send.at[4 + w], recv_sem=recv.at[4 + w],
            device_id={"cross": walls[w][1]}, device_id_type=MESH,
        )

    def corner_in(w, s):
        return pltpu.make_async_remote_copy(
            src_ref=yp.at[w], dst_ref=cp.at[s, w], send_sem=send.at[6 + 2 * w + s],
            recv_sem=recv.at[6 + 2 * w + s], device_id={"slab": sides[s][1]}, device_id_type=MESH,
        )

    def x_in(s):
        pairs = ((visc.at[pl.ds(0, 3)], vx.at[s]), (forc.at[:, pl.ds(0, 2)], fx.at[s]))
        return [
            pltpu.make_async_remote_copy(
                src_ref=a, dst_ref=b, send_sem=send.at[2 * s + n], recv_sem=recv.at[2 * s + n],
                device_id={"slab": sides[s][1]}, device_id_type=MESH,
            )
            for n, (a, b) in enumerate(pairs)
        ]

    for w in range(2):

        @pl.when(walls[w][2])
        def _():
            y_copy(w).start()

    for s in range(2):

        @pl.when(sides[s][2])
        def _():
            for copy in x_copies(s):
                copy.start()

    for w in range(2):

        @pl.when(walls[w][2])
        def _():
            y_in(w).wait_recv()
            for s in range(2):

                @pl.when(sides[s][2])
                def _():
                    corner_copy(w, s).start()

    for s in range(2):

        @pl.when(sides[s][2])
        def _():
            for copy in x_in(s):
                copy.wait_recv()
            for copy in x_copies(s):
                copy.wait_send()

    for w in range(2):

        @pl.when(walls[w][2])
        def _():
            y_copy(w).wait_send()
            for s in range(2):

                @pl.when(sides[s][2])
                def _():
                    corner_in(w, s).wait_recv()
                    corner_copy(w, s).wait_send()


def halos(viscosity, forcing, sn, cn):
    nx, ny, nz = viscosity.shape
    f32 = jnp.float32

    def packed(v0, f0):
        a = viscosity[:, v0 : v0 + 3].reshape(3 * nx, nz)
        b = forcing[:, :, f0 : f0 + 2].reshape(4 * nx, nz)
        return jnp.concatenate([a, b], 0)

    ypack = jnp.stack([packed(0, 0), packed(ny - 3, ny - 2)])
    anywhere = pl.BlockSpec(memory_space=pl.ANY)
    vx, fx, yp, cp = pl.pallas_call(
        functools.partial(halo_body, sn, cn),
        out_shape=(
            jax.ShapeDtypeStruct((2, 3, ny, nz), f32),
            jax.ShapeDtypeStruct((2, 2, 2, ny, nz), f32),
            jax.ShapeDtypeStruct((2, 7 * nx, nz), f32),
            jax.ShapeDtypeStruct((2, 2, 7 * nx, nz), f32),
        ),
        in_specs=[anywhere] * 3,
        out_specs=(anywhere,) * 4,
        scratch_shapes=[pltpu.SemaphoreType.DMA((10,)), pltpu.SemaphoreType.DMA((10,))],
        compiler_params=pltpu.CompilerParams(collective_id=1, has_side_effects=True),
        name="halos",
    )(viscosity, forcing, ypack)
    slab, cross = lax.axis_index("slab"), lax.axis_index("cross")
    side = (slab > 0, slab < sn - 1)
    wall = (cross > 0, cross < cn - 1)

    def only(cond, a):
        return jnp.where(cond, a, 0.0)

    def unpacked(p):
        return p[: 3 * nx].reshape(nx, 3, nz), p[3 * nx :].reshape(2, nx, 2, nz)

    yv, yf = zip(*[unpacked(only(wall[w], yp[w])) for w in range(2)])
    vs, fs = [jnp.concatenate([yv[0], viscosity, yv[1]], 1)], [jnp.concatenate([yf[0], forcing, yf[1]], 2)]
    for s in range(2):
        cv, cf = zip(*[unpacked(only(side[s] & wall[w], cp[s, w])) for w in range(2)])
        vcut, fcut = ((nx - 3, nx), (nx - 2, nx)) if s == 0 else ((0, 3), (0, 2))
        cv = [a[vcut[0] : vcut[1]] for a in cv]
        cf = [a[:, fcut[0] : fcut[1]] for a in cf]
        vs.append(jnp.concatenate([cv[0], only(side[s], vx[s]), cv[1]], 1))
        fs.append(jnp.concatenate([cf[0], only(side[s], fx[s]), cf[1]], 2))
    return jnp.concatenate([vs[1], vs[0], vs[2]], 0), jnp.concatenate([fs[1], fs[0], fs[2]], 1)


def zs(a, s):
    if s > 0:
        return jnp.pad(a[..., s:], [(0, 0)] * (a.ndim - 1) + [(0, s)])
    return jnp.pad(a[..., :s], [(0, 0)] * (a.ndim - 1) + [(-s, 0)])


def shards(forcing, viscosity, owner_slot):
    w0, w1, w2 = cheb_weights()
    slab_n, cross_n = lax.axis_size("slab"), lax.axis_size("cross")
    slab, cross = lax.axis_index("slab"), lax.axis_index("cross")
    nx, ny, nz = viscosity.shape
    v, f = lax.optimization_barrier(halos(viscosity, forcing, slab_n, cross_n))
    c = v[1:-1, 1:-1]
    fxp, fxm = 0.5 * (c + v[2:, 1:-1]), 0.5 * (c + v[:-2, 1:-1])
    fyp, fym = 0.5 * (c + v[1:-1, 2:]), 0.5 * (c + v[1:-1, :-2])
    fzp, fzm = 0.5 * (c + zs(c, 1)), 0.5 * (c + zs(c, -1))
    diag = fxp + fxm + fyp + fym + fzp + fzm
    xi = lax.broadcasted_iota(jnp.int32, c.shape, 0) + slab * nx - 2
    yi = lax.broadcasted_iota(jnp.int32, c.shape, 1) + cross * ny - 2
    inside = (xi >= 0) & (xi < nx * slab_n) & (yi >= 0) & (yi < ny * cross_n)
    dinv = jnp.where(inside, 1.0 / jnp.where(inside, diag, 1.0), 0.0)

    def inner(a):
        return a[..., 1:-1, 1:-1, :]

    def nbr(a, dx, dy):
        n1, n2 = a.shape[-3], a.shape[-2]
        return a[..., 1 + dx : n1 - 1 + dx, 1 + dy : n2 - 1 + dy, :]

    faces2 = (fxp, fxm, fyp, fym, fzp, fzm)
    faces1 = tuple(inner(a) for a in faces2)
    faces0 = tuple(inner(a) for a in faces1)
    d1, d0 = inner(dinv), inner(inner(dinv))

    def tapply(y, fc, di):
        fxp, fxm, fyp, fym, fzp, fzm = fc
        yc = inner(y)
        return di * (
            fxp * nbr(y, 1, 0) + fxm * nbr(y, -1, 0) + fyp * nbr(y, 0, 1)
            + fym * nbr(y, 0, -1) + fzp * zs(yc, 1) + fzm * zs(yc, -1)
        )

    y0 = dinv * f
    t1 = tapply(y0, faces1, d1)
    free = w0 * inner(inner(y0)) + tapply(w1 * inner(y0) + w2 * t1, faces0, d0)

    xp, xm, yp, ym, zp, zm = faces1
    W = {
        (0, 0): d1 * (yp * nbr(dinv, 0, 1) + ym * nbr(dinv, 0, -1)),
        (1, 0): d1 * xp * nbr(dinv, 1, 0),
        (-1, 0): d1 * xm * nbr(dinv, -1, 0),
        (0, 1): d1 * zp * zs(d1, 1),
        (0, -1): d1 * zm * zs(d1, -1),
    }
    U = {o: w2 * a for o, a in W.items()}
    U[(0, 0)] = U[(0, 0)] + w1 * d1
    xp, xm, yp, ym, zp, zm = faces0
    acc = {}

    def add(o, a):
        acc[o] = acc[o] + a if o in acc else a

    for o, a in U.items():
        ac = inner(a)
        add(o, yp * nbr(a, 0, 1) + ym * nbr(a, 0, -1))
        add((o[0] + 1, o[1]), xp * nbr(a, 1, 0))
        add((o[0] - 1, o[1]), xm * nbr(a, -1, 0))
        add((o[0], o[1] + 1), zp * zs(ac, 1))
        add((o[0], o[1] - 1), zm * zs(ac, -1))
    m = {o: d0 * a for o, a in acc.items()}
    m[(0, 0)] = m[(0, 0)] + w0 * d0

    part = jnp.stack([jnp.sum(m[o], axis=1) for o in OFFSETS] + [jnp.sum(free[0], 1), jnp.sum(free[1], 1)], 0)
    gs, pressure = column_cg(part, owner_slot.reshape(1, nz), slab_n, cross_n)
    velocity = free
    for o, a in m.items():
        s = gs[2 + o[1], :, 2 + o[0] : 2 + o[0] + nx]
        velocity = velocity - a[None] * s[:, :, None, :]
    return velocity, pressure


def solution(mesh):
    in_specs = (P(None, "slab", "cross", None), P("slab", "cross", None), P())
    out_specs = (P(None, "slab", "cross", None), P("slab", "cross"))
    return jax.shard_map(shards, mesh=mesh, in_specs=in_specs, out_specs=out_specs, check_vma=False)
```

```python
import functools

import jax
import jax.numpy as jnp
from jax import lax
from jax.experimental import pallas as pl
from jax.experimental.pallas import tpu as pltpu
from jax.sharding import PartitionSpec as P

MESH = pl.DeviceIdType.MESH

OUTER = 2
DEGREE = 3


cheb_theta = 1.025
cheb_delta = 0.975


def cheb_weights():
    sigma = cheb_theta / cheb_delta
    solved = [1.0 / cheb_theta] + [0.0] * (DEGREE - 1)
    change = list(solved)
    rho_prev = 1.0 / sigma
    for step in range(DEGREE - 1):
        resid = [(1.0 if k == 0 else solved[k - 1]) - solved[k] for k in range(DEGREE)]
        resid[0] = 1.0 - solved[0]
        rho = 1.0 / (2.0 * sigma - rho_prev)
        change = [rho * rho_prev * c + 2.0 * rho / cheb_delta * r for c, r in zip(change, resid)]
        solved = [s + c for s, c in zip(solved, change)]
        rho_prev = rho
    return solved


OFFSETS = [(0, 0), (1, 0), (0, 1), (2, 0), (0, 2), (1, 1), (1, -1)]


def moved(a, dx, dz):
    n0, n1 = a.shape
    if dx:
        row = lax.broadcasted_iota(jnp.int32, a.shape, 0)
        a = jnp.where((row + dx >= 0) & (row + dx < n0), pltpu.roll(a, (-dx) % n0, 0), 0.0)
    if dz:
        col = lax.broadcasted_iota(jnp.int32, a.shape, 1)
        a = jnp.where((col + dz >= 0) & (col + dz < n1), pltpu.roll(a, (-dz) % n1, 1), 0.0)
    return a


def cg_body(sn, cn, part, owner, gs, press, crecv, kall, kfull, back, gpad, csend, crecv_sem, ssend, srecv):
    slab, cross = lax.axis_index("slab"), lax.axis_index("cross")
    nf, nx, nz = part.shape
    barrier = pltpu.get_barrier_semaphore()
    for d in range(1, cn):
        pl.semaphore_signal(barrier, inc=1, device_id={"cross": lax.rem(cross + d, cn)}, device_id_type=MESH)
    zn = sn // 2
    place, core = slab // 2, lax.rem(slab, 2)
    for d in range(1, zn):
        pl.semaphore_signal(
            barrier, inc=1, device_id={"slab": lax.rem(place + d, zn) * 2 + core}, device_id_type=MESH
        )
    partner = place * 2 + 1 - core
    pl.semaphore_signal(barrier, inc=1, device_id={"slab": partner}, device_id_type=MESH)
    pl.semaphore_wait(barrier, cn - 1 + zn)
    copies = []
    for d in range(1, cn):
        copy = pltpu.make_async_remote_copy(
            src_ref=part, dst_ref=crecv.at[cross], send_sem=csend.at[d - 1], recv_sem=crecv_sem.at[d - 1],
            device_id={"cross": lax.rem(cross + d, cn)}, device_id_type=MESH,
        )
        copy.start()
        copies.append(copy)
    crecv[cross] = part[...]
    for copy in copies:
        copy.wait()
    for n in range(nf):
        total = crecv[0, n]
        for d in range(1, cn):
            total = total + crecv[d, n]
        kall[slab, n] = total
    def pass_on(block, target, sem):
        copy = pltpu.make_async_remote_copy(
            src_ref=kall.at[block], dst_ref=kall.at[block], send_sem=ssend.at[sem], recv_sem=srecv.at[sem],
            device_id={"slab": target}, device_id_type=MESH,
        )
        copy.start()
        return copy

    far = [pass_on(slab, lax.rem(place + d, zn) * 2 + core, d - 1) for d in range(1, zn)]
    near = [pass_on(slab, partner, zn - 1)]
    for d in range(1, zn):
        far[d - 1].wait_recv()
        near.append(pass_on(lax.rem(place - d + zn, zn) * 2 + core, partner, zn - 1 + d))
    for copy in near:
        copy.wait()
    for copy in far:
        copy.wait_send()
    for n in range(nf):
        for s in range(sn):
            kfull[n, s * nx : (s + 1) * nx, :] = kall[s, n]
    for n, o in enumerate(OFFSETS[1:]):
        back[n] = moved(kfull[n + 1], -o[0], -o[1])

    def diverge(cx, cz):
        return cx - moved(cx, -1, 0) + cz - moved(cz, 0, -1)

    def kapply(q):
        out = kfull[0] * q
        for n, o in enumerate(OFFSETS[1:]):
            out = out + kfull[n + 1] * moved(q, o[0], o[1]) + back[n] * moved(q, -o[0], -o[1])
        return out

    def grad(q):
        return q - moved(q, 1, 0), q - moved(q, 0, 1)

    target = diverge(kfull[nf - 2], kfull[nf - 1])
    pressure = jnp.zeros_like(target)
    resid = dirn = target
    rr = jnp.sum(resid * resid)
    for step in range(OUTER):
        gx, gz = grad(dirn)
        image = diverge(kapply(gx), kapply(gz))
        alpha = rr / jnp.sum(dirn * image)
        pressure = pressure + alpha * dirn
        if step + 1 < OUTER:
            resid = resid - alpha * image
            fresh = jnp.sum(resid * resid)
            dirn = resid + (fresh / rr) * dirn
            rr = fresh
    zero = jnp.zeros((8, nz), jnp.float32)
    full = sn * nx
    for c, q in enumerate(grad(pressure)):
        for dz in range(-2, 3):
            gpad[dz + 2, c, 0:8, :] = zero
            gpad[dz + 2, c, full + 8 : full + 16, :] = zero
            gpad[dz + 2, c, 8 : full + 8, :] = moved(q, 0, dz)
    kfull[0] = pressure
    width = press.shape[1]
    slot = lax.broadcasted_iota(jnp.int32, (width, nz), 0) + cross * width
    onehot = (jnp.broadcast_to(owner[...], (width, nz)) == slot).astype(jnp.float32)
    for s in range(sn):

        @pl.when(slab == s)
        def _():
            gs[...] = gpad[:, :, 6 + s * nx : 10 + (s + 1) * nx, :]
            press[...] = lax.dot_general(
                kfull[0, s * nx : (s + 1) * nx, :], onehot, (((1,), (1,)), ((), ())),
                precision=lax.Precision.HIGHEST, preferred_element_type=jnp.float32,
            )


def column_cg(part, owner, sn, cn):
    nf, nx, nz = part.shape
    f32 = jnp.float32
    vmem = pl.BlockSpec(memory_space=pltpu.VMEM)
    return pl.pallas_call(
        functools.partial(cg_body, sn, cn),
        out_shape=(
            jax.ShapeDtypeStruct((5, 2, nx + 4, nz), f32),
            jax.ShapeDtypeStruct((nx, nz // cn), f32),
        ),
        in_specs=[vmem, vmem],
        out_specs=(vmem, vmem),
        scratch_shapes=[
            pltpu.VMEM((cn, nf, nx, nz), f32),
            pltpu.VMEM((sn, nf, nx, nz), f32),
            pltpu.VMEM((nf, sn * nx, nz), f32),
            pltpu.VMEM((nf - 3, sn * nx, nz), f32),
            pltpu.VMEM((5, 2, sn * nx + 16, nz), f32),
            pltpu.SemaphoreType.DMA((cn - 1,)),
            pltpu.SemaphoreType.DMA((cn - 1,)),
            pltpu.SemaphoreType.DMA((sn - 1,)),
            pltpu.SemaphoreType.DMA((sn - 1,)),
        ],
        compiler_params=pltpu.CompilerParams(collective_id=0, has_side_effects=True),
        name="column_cg",
    )(part, owner)


def subtract_body(keys, gs, free, *refs):
    fields, out = refs[:-1], refs[-1]
    comps, nx = free.shape[0], free.shape[1]
    for i in range(nx):
        total = [free[c, i] for c in range(comps)]
        for (dx, dz), field in zip(keys, fields):
            a = field[i]
            for c in range(comps):
                total[c] = total[c] - a * gs[2 + dz, c, 2 + dx + i : 3 + dx + i, :]
        for c in range(comps):
            out[c, i] = total[c]


def subtract_gradient(gs, free, m):
    comps, nx, ny, nz = free.shape
    step = 16
    keys = list(m)
    wide = pl.BlockSpec((comps, nx, step, nz), lambda j: (0, 0, j, 0))
    one = pl.BlockSpec((nx, step, nz), lambda j: (0, j, 0))
    whole = pl.BlockSpec(gs.shape, lambda j: (0, 0, 0, 0))
    return pl.pallas_call(
        functools.partial(subtract_body, keys),
        grid=(ny // step,),
        out_shape=jax.ShapeDtypeStruct(free.shape, jnp.float32),
        in_specs=[whole, wide] + [one] * len(keys),
        out_specs=wide,
        name="subtract_gradient",
    )(gs, free, *[m[o] for o in keys])


def halo_body(sn, cn, visc, forc, ypack, vx, fx, yp, cp, send, recv):
    slab, cross = lax.axis_index("slab"), lax.axis_index("cross")
    nx = visc.shape[0]
    sides = (("slab", slab - 1, slab > 0), ("slab", slab + 1, slab < sn - 1))
    walls = (("cross", cross - 1, cross > 0), ("cross", cross + 1, cross < cn - 1))
    barrier = pltpu.get_barrier_semaphore()
    for axis, peer, there in sides + walls:

        @pl.when(there)
        def _():
            pl.semaphore_signal(barrier, inc=1, device_id={axis: peer}, device_id_type=MESH)

    around = [jnp.where(there, 1, 0) for axis, peer, there in sides + walls]
    pl.semaphore_wait(barrier, around[0] + around[1] + around[2] + around[3])

    def x_copies(s):
        axis, peer, there = sides[s]
        v0, f0 = (0, 0) if s == 0 else (nx - 3, nx - 2)
        pairs = ((visc.at[pl.ds(v0, 3)], vx.at[1 - s]), (forc.at[:, pl.ds(f0, 2)], fx.at[1 - s]))
        return [
            pltpu.make_async_remote_copy(
                src_ref=a, dst_ref=b, send_sem=send.at[2 * s + n], recv_sem=recv.at[2 * (1 - s) + n],
                device_id={axis: peer}, device_id_type=MESH,
            )
            for n, (a, b) in enumerate(pairs)
        ]

    def y_copy(w):
        axis, peer, there = walls[w]
        return pltpu.make_async_remote_copy(
            src_ref=ypack.at[w], dst_ref=yp.at[1 - w], send_sem=send.at[4 + w], recv_sem=recv.at[4 + 1 - w],
            device_id={axis: peer}, device_id_type=MESH,
        )

    def corner_copy(w, s):
        axis, peer, there = sides[s]
        return pltpu.make_async_remote_copy(
            src_ref=yp.at[w], dst_ref=cp.at[1 - s, w], send_sem=send.at[6 + 2 * w + s],
            recv_sem=recv.at[6 + 2 * w + 1 - s], device_id={axis: peer}, device_id_type=MESH,
        )

    def y_in(w):
        return pltpu.make_async_remote_copy(
            src_ref=ypack.at[w], dst_ref=yp.at[w], send_sem=send.at[4 + w], recv_sem=recv.at[4 + w],
            device_id={"cross": walls[w][1]}, device_id_type=MESH,
        )

    def corner_in(w, s):
        return pltpu.make_async_remote_copy(
            src_ref=yp.at[w], dst_ref=cp.at[s, w], send_sem=send.at[6 + 2 * w + s],
            recv_sem=recv.at[6 + 2 * w + s], device_id={"slab": sides[s][1]}, device_id_type=MESH,
        )

    def x_in(s):
        pairs = ((visc.at[pl.ds(0, 3)], vx.at[s]), (forc.at[:, pl.ds(0, 2)], fx.at[s]))
        return [
            pltpu.make_async_remote_copy(
                src_ref=a, dst_ref=b, send_sem=send.at[2 * s + n], recv_sem=recv.at[2 * s + n],
                device_id={"slab": sides[s][1]}, device_id_type=MESH,
            )
            for n, (a, b) in enumerate(pairs)
        ]

    for w in range(2):

        @pl.when(walls[w][2])
        def _():
            y_copy(w).start()

    for s in range(2):

        @pl.when(sides[s][2])
        def _():
            for copy in x_copies(s):
                copy.start()

    for w in range(2):

        @pl.when(walls[w][2])
        def _():
            y_in(w).wait_recv()
            for s in range(2):

                @pl.when(sides[s][2])
                def _():
                    corner_copy(w, s).start()

    for s in range(2):

        @pl.when(sides[s][2])
        def _():
            for copy in x_in(s):
                copy.wait_recv()
            for copy in x_copies(s):
                copy.wait_send()

    for w in range(2):

        @pl.when(walls[w][2])
        def _():
            y_copy(w).wait_send()
            for s in range(2):

                @pl.when(sides[s][2])
                def _():
                    corner_in(w, s).wait_recv()
                    corner_copy(w, s).wait_send()


def halos(viscosity, forcing, sn, cn):
    nx, ny, nz = viscosity.shape
    f32 = jnp.float32

    def packed(v0, f0):
        a = viscosity[:, v0 : v0 + 3].reshape(3 * nx, nz)
        b = forcing[:, :, f0 : f0 + 2].reshape(4 * nx, nz)
        return jnp.concatenate([a, b], 0)

    ypack = jnp.stack([packed(0, 0), packed(ny - 3, ny - 2)])
    anywhere = pl.BlockSpec(memory_space=pl.ANY)
    vx, fx, yp, cp = pl.pallas_call(
        functools.partial(halo_body, sn, cn),
        out_shape=(
            jax.ShapeDtypeStruct((2, 3, ny, nz), f32),
            jax.ShapeDtypeStruct((2, 2, 2, ny, nz), f32),
            jax.ShapeDtypeStruct((2, 7 * nx, nz), f32),
            jax.ShapeDtypeStruct((2, 2, 7 * nx, nz), f32),
        ),
        in_specs=[anywhere] * 3,
        out_specs=(anywhere,) * 4,
        scratch_shapes=[pltpu.SemaphoreType.DMA((10,)), pltpu.SemaphoreType.DMA((10,))],
        compiler_params=pltpu.CompilerParams(collective_id=1, has_side_effects=True),
        name="halos",
    )(viscosity, forcing, ypack)
    slab, cross = lax.axis_index("slab"), lax.axis_index("cross")
    side = (slab > 0, slab < sn - 1)
    wall = (cross > 0, cross < cn - 1)

    def only(cond, a):
        return jnp.where(cond, a, 0.0)

    def unpacked(p):
        return p[: 3 * nx].reshape(nx, 3, nz), p[3 * nx :].reshape(2, nx, 2, nz)

    yv, yf = zip(*[unpacked(only(wall[w], yp[w])) for w in range(2)])
    vs, fs = [jnp.concatenate([yv[0], viscosity, yv[1]], 1)], [jnp.concatenate([yf[0], forcing, yf[1]], 2)]
    for s in range(2):
        cv, cf = zip(*[unpacked(only(side[s] & wall[w], cp[s, w])) for w in range(2)])
        vcut, fcut = ((nx - 3, nx), (nx - 2, nx)) if s == 0 else ((0, 3), (0, 2))
        cv = [a[vcut[0] : vcut[1]] for a in cv]
        cf = [a[:, fcut[0] : fcut[1]] for a in cf]
        vs.append(jnp.concatenate([cv[0], only(side[s], vx[s]), cv[1]], 1))
        fs.append(jnp.concatenate([cf[0], only(side[s], fx[s]), cf[1]], 2))
    return jnp.concatenate([vs[1], vs[0], vs[2]], 0), jnp.concatenate([fs[1], fs[0], fs[2]], 1)


def zs(a, s):
    if s > 0:
        return jnp.pad(a[..., s:], [(0, 0)] * (a.ndim - 1) + [(0, s)])
    return jnp.pad(a[..., :s], [(0, 0)] * (a.ndim - 1) + [(-s, 0)])


def shards(forcing, viscosity, owner_slot):
    w0, w1, w2 = cheb_weights()
    slab_n, cross_n = lax.axis_size("slab"), lax.axis_size("cross")
    slab, cross = lax.axis_index("slab"), lax.axis_index("cross")
    nx, ny, nz = viscosity.shape
    v, f = lax.optimization_barrier(halos(viscosity, forcing, slab_n, cross_n))
    c = v[1:-1, 1:-1]
    fxp, fxm = 0.5 * (c + v[2:, 1:-1]), 0.5 * (c + v[:-2, 1:-1])
    fyp, fym = 0.5 * (c + v[1:-1, 2:]), 0.5 * (c + v[1:-1, :-2])
    fzp, fzm = 0.5 * (c + zs(c, 1)), 0.5 * (c + zs(c, -1))
    diag = fxp + fxm + fyp + fym + fzp + fzm
    xi = lax.broadcasted_iota(jnp.int32, c.shape, 0) + slab * nx - 2
    yi = lax.broadcasted_iota(jnp.int32, c.shape, 1) + cross * ny - 2
    inside = (xi >= 0) & (xi < nx * slab_n) & (yi >= 0) & (yi < ny * cross_n)
    dinv = jnp.where(inside, 1.0 / jnp.where(inside, diag, 1.0), 0.0)

    def inner(a):
        return a[..., 1:-1, 1:-1, :]

    def nbr(a, dx, dy):
        n1, n2 = a.shape[-3], a.shape[-2]
        return a[..., 1 + dx : n1 - 1 + dx, 1 + dy : n2 - 1 + dy, :]

    faces2 = (fxp, fxm, fyp, fym, fzp, fzm)
    faces1 = tuple(inner(a) for a in faces2)
    faces0 = tuple(inner(a) for a in faces1)
    d1, d0 = inner(dinv), inner(inner(dinv))

    def tapply(y, fc, di):
        fxp, fxm, fyp, fym, fzp, fzm = fc
        yc = inner(y)
        return di * (
            fxp * nbr(y, 1, 0) + fxm * nbr(y, -1, 0) + fyp * nbr(y, 0, 1)
            + fym * nbr(y, 0, -1) + fzp * zs(yc, 1) + fzm * zs(yc, -1)
        )

    y0 = dinv * f
    t1 = tapply(y0, faces1, d1)
    free = w0 * inner(inner(y0)) + tapply(w1 * inner(y0) + w2 * t1, faces0, d0)

    xp, xm, yp, ym, zp, zm = faces1
    W = {
        (0, 0): d1 * (yp * nbr(dinv, 0, 1) + ym * nbr(dinv, 0, -1)),
        (1, 0): d1 * xp * nbr(dinv, 1, 0),
        (-1, 0): d1 * xm * nbr(dinv, -1, 0),
        (0, 1): d1 * zp * zs(d1, 1),
        (0, -1): d1 * zm * zs(d1, -1),
    }
    U = {o: w2 * a for o, a in W.items()}
    U[(0, 0)] = U[(0, 0)] + w1 * d1
    xp, xm, yp, ym, zp, zm = faces0
    acc = {}

    def add(o, a):
        acc[o] = acc[o] + a if o in acc else a

    for o, a in U.items():
        ac = inner(a)
        add(o, yp * nbr(a, 0, 1) + ym * nbr(a, 0, -1))
        add((o[0] + 1, o[1]), xp * nbr(a, 1, 0))
        add((o[0] - 1, o[1]), xm * nbr(a, -1, 0))
        add((o[0], o[1] + 1), zp * zs(ac, 1))
        add((o[0], o[1] - 1), zm * zs(ac, -1))
    m = {o: d0 * a for o, a in acc.items()}
    m[(0, 0)] = m[(0, 0)] + w0 * d0

    part = jnp.stack([jnp.sum(m[o], axis=1) for o in OFFSETS] + [jnp.sum(free[0], 1), jnp.sum(free[1], 1)], 0)
    gs, pressure = column_cg(part, owner_slot.reshape(1, nz), slab_n, cross_n)
    velocity = subtract_gradient(gs, free, m)
    return velocity, pressure


def solution(mesh):
    in_specs = (P(None, "slab", "cross", None), P("slab", "cross", None), P())
    out_specs = (P(None, "slab", "cross", None), P("slab", "cross"))
    return jax.shard_map(shards, mesh=mesh, in_specs=in_specs, out_specs=out_specs, check_vma=False)
```
